256 devices in a mesh: scen: 16 (over z_lo, y, core), tm: 16 (over z_hi, x).
Axes of the slice: x: 4, y: 4, z: 8 (z_hi: 4, z_lo: 2; z = z_hi * 2 + z_lo), core: 2. Of those that a mesh axis runs over, the one named last changes fastest.
Arguments:
- cotangent: float32 [64, 336, 2048], P('scen', 'tm'), may hold values from -6 to 6
- blocks: bfloat16 [16, 6, 128, 128], P('tm'), may hold values from -0.21875 to 0.21875
- zone_links: int32 [16, 6], replicated, may hold values from 0 to 15, as said below
- step_size: float32 [2048], replicated, may hold values from 0.3 to 1
- coupling: bfloat16 [16, 336, 336], P('tm'), may hold values from -0.3125 to 0.3125
- ramp_band: int32 [16], P('tm'), may hold values from 42 to 336, as said below
- candidates: int32 [2048], P('scen'), may hold values from 0 to 2047, as said below
Outputs:
- initial_adjoint: float32 [64, 336, 2048], P('scen', 'tm')
- siting_gradient: float32 [336, 2048], P('tm', 'scen')
The draws below stay inside these ranges and needn't reach their ends.
Inputs may be any that keep to these rules, and one draw needn't show every extreme that they name: zone_links[z, 0] = z, and the 6 entries of a row are distinct zones. `ramp_band`: at least one zone has reach 336. `candidates`: the entries of block m of 128 consecutive entries are distinct buses in m * (128) to (m + 1) * 128 - 1.
All inputs are finite; a program needn't handle non-finite values.
Results may differ from the reference program's by a relative error of at most 0.0029.
Values may be sent and summed in bfloat16 or wider, within the bound.
No kernel may reach another device: no remote copies, remote signals or barrier semaphores. Data moves between devices by JAX's collectives and lax.ppermute only.
A program may use at most 64 MiB of HBM per device.

```python
import math
import jax
import jax.numpy as jnp
from jax import lax

BUS = 128
HOURS = 336
NBR = 6
SWEEPS = 2
CAND_DEV = 128
ZONES = 16
NB = 2048
SCENS = 64
CANDS = 2048


def draw_zone_links(key, part):
    keys = jax.random.split(key, ZONES)
    others = jax.vmap(lambda k: jax.random.permutation(k, ZONES - 1)[:NBR - 1])(keys)
    zone_ids = jnp.arange(ZONES, dtype=jnp.int32)
    rest = (zone_ids[:, None] + 1 + others.astype(jnp.int32)) % ZONES
    return jnp.concatenate([zone_ids[:, None], rest], axis=1).astype(jnp.int32)


def draw_ramp_band(key, part):
    first, second = jax.random.split(key)
    band = jax.random.randint(first, (ZONES,), HOURS // 8, HOURS + 1).astype(jnp.int32)
    widest = jax.random.randint(second, (), 0, ZONES)
    return band.at[widest].set(HOURS).astype(jnp.int32)


def draw_candidates(key, part):
    groups = CANDS // CAND_DEV
    width = NB // groups
    keys = jax.random.split(key, groups)
    chosen = jax.vmap(lambda k: jax.random.permutation(k, width)[:CAND_DEV])(keys).astype(jnp.int32)
    offsets = (jnp.arange(groups, dtype=jnp.int32) * width)[:, None]
    return (chosen + offsets).reshape(CANDS).astype(jnp.int32)


def strengthened(values, key, source, target, blocks, factor):
    def block_of(dim):
        return (jnp.arange(values.shape[dim]) // (values.shape[dim] // blocks)).reshape((-1,) + (1,) * (values.ndim - 1 - dim))

    one_side = jax.random.permutation(key, blocks)[block_of(target)]
    second = (block_of(target) + blocks // 2) % blocks
    return jnp.where((block_of(source) == one_side) | (block_of(source) == second), factor * values, values)


def steps_of(stream_key, extent, cuts, smallest, top_value):
    gain = 1.0
    for axis_at, blocks in cuts:
        heights = jax.random.uniform(jax.random.fold_in(jax.random.fold_in(stream_key, 6), axis_at), (blocks,), jnp.float32, smallest / len(cuts), top_value / len(cuts))
        gain = gain * jnp.repeat(jnp.exp(heights), extent[axis_at] // blocks).reshape((-1,) + (1,) * (len(extent) - 1 - axis_at))
    return gain


def centred(rng, extent, scale, bound, cuts=(), held_as=jnp.bfloat16):
    values = jax.random.normal(rng, extent, jnp.float32) * scale
    if len(cuts) > 0:
        values = steps_of(rng, extent, cuts, -0.22, 0.18) * values
    return jnp.clip(values, min=-bound, max=bound).astype(held_as)


def gaussian_with(own_key, shape, scale, reach, pieces, heavy, kind=jnp.bfloat16):
    values = scale * jax.random.normal(own_key, shape, jnp.float32)
    if pieces:
        values = values * steps_of(own_key, shape, pieces, -0.22, 0.18)
    return jnp.clip(strengthened(values, jax.random.fold_in(own_key, 3), *heavy), -reach, reach).astype(kind)


def setup_inputs(seed: int = 0) -> dict:
    arg_keys = jax.random.split(jax.random.key(seed), 8)
    cotangent = gaussian_with(arg_keys[0], (SCENS, HOURS, NB), 1.0, 6.0, ((0, 16), (1, 16)), (0, 2, 16, 2.0), jnp.float32)
    blocks = centred(arg_keys[1], (ZONES, NBR, BUS, BUS), (NBR * BUS) ** -0.5, 0.21875, ((0, 16),))
    zone_links = draw_zone_links(jax.random.fold_in(arg_keys[7], 71), 0)
    step_size = jnp.clip(jnp.exp(jax.random.uniform(arg_keys[3], (NB,), jnp.float32, math.log(0.3), math.log(1.0))), 0.3, 1.0)
    coupling = centred(arg_keys[4], (ZONES, HOURS, HOURS), HOURS ** -0.5, 0.3125, ((0, 16),))
    ramp_band = draw_ramp_band(jax.random.fold_in(arg_keys[7], 71), 0)
    candidates = draw_candidates(jax.random.fold_in(arg_keys[7], 71), 0)
    return dict(cotangent=cotangent, blocks=blocks, zone_links=zone_links, step_size=step_size, coupling=coupling, ramp_band=ramp_band, candidates=candidates)


def reference(cotangent, blocks, zone_links, step_size, coupling, ramp_band, candidates):
    hour_ids = jnp.arange(HOURS, dtype=jnp.int32)
    spread = jnp.abs(hour_ids[:, None] - hour_ids[None, :])
    masked = jnp.where(spread[None, :, :] <= ramp_band[:, None, None], coupling, jnp.zeros_like(coupling))
    blocks_wide = blocks.astype(jnp.float32)
    masked_wide = masked.astype(jnp.float32)

    def one_scenario(adjoint):
        grad_part = jnp.zeros((HOURS, NB), jnp.float32)
        for sweep in range(SWEEPS):
            weighted = adjoint * step_size[None, :]
            grad_part = grad_part + weighted
            scaled = weighted.astype(jnp.bfloat16)
            panel = scaled.astype(jnp.float32).reshape(HOURS, ZONES, BUS)
            picked = panel[:, zone_links, :]
            network = jnp.einsum("tzki,zkij->tzj", picked, blocks_wide).reshape(HOURS, NB)
            temporal = jnp.einsum("ztu,tzi->uzi", masked_wide, panel).reshape(HOURS, NB)
            temporal = temporal.astype(jnp.bfloat16).astype(jnp.float32)
            adjoint = adjoint - network - temporal
        return adjoint, grad_part

    def step_fn(total, adjoint):
        result, grad_part = one_scenario(adjoint)
        return total + grad_part, result

    total, initial_adjoint = lax.scan(step_fn, jnp.zeros((HOURS, NB), jnp.float32), cotangent)
    grad = total * (1.0 / SCENS)
    siting_gradient = grad[:, candidates]
    return initial_adjoint, siting_gradient
```

```python
import jax
import jax.numpy as jnp
from jax import lax
from jax.experimental import pallas as pl
from jax.experimental.pallas import tpu as pltpu
from jax.sharding import Mesh
from jax.sharding import PartitionSpec as P

SCEN = ("z_lo", "y", "core")
TM = ("z_hi", "x")
F32, BF16 = jnp.float32, jnp.bfloat16
VMEM_LIMIT = 48 * 1024 * 1024


def call(body, outs, scratch=(), specs=None, **kw):
    return pl.pallas_call(
        body,
        out_shape=outs,
        in_specs=specs,
        scratch_shapes=list(scratch),
        compiler_params=pltpu.CompilerParams(vmem_limit_bytes=VMEM_LIMIT),
        **kw,
    )


VM = pl.BlockSpec(memory_space=pltpu.VMEM)
SM = pl.BlockSpec(memory_space=pltpu.SMEM)
ANY = pl.BlockSpec(memory_space=pl.ANY)


def scale_body(place, cot, step, blocks, sent, grad, rows):
    hours, scens, buses = cot.shape
    zones, width = sent.shape[0], sent.shape[2]
    piece = sent.shape[1] - hours * scens
    for hour in range(hours):
        weighted = cot[hour] * step[...]
        rows[scens * hour : scens * (hour + 1), :] = weighted
        grad[hour : hour + 1, :] = jnp.sum(weighted, axis=0, keepdims=True)
    first = pl.multiple_of(place[0] * piece, 16)
    own = blocks[pl.ds(first, piece), :]
    for zone in range(zones):
        sent[zone, 0:piece, :] = own
        sent[zone, piece:, :] = rows[:, width * zone : width * (zone + 1)].astype(BF16)


def temporal_body(skip, band, got, coupling, out, rows):
    zones, count, width = out.shape
    total = coupling.shape[0]
    scens = zones * count // total
    for zone in range(zones):
        rows[count * zone : count * (zone + 1), :] = got[zone, skip:, :].astype(F32)
    hours = jnp.concatenate(
        [rows[pl.ds(scen, total, stride=scens), :].astype(BF16) for scen in range(scens)], axis=1
    )
    spread = jnp.abs(
        lax.broadcasted_iota(jnp.int32, (total, total), 0)
        - lax.broadcasted_iota(jnp.int32, (total, total), 1)
    )
    masked = jnp.where(spread <= band[0], coupling[...].astype(F32), 0.0).astype(BF16)
    result = lax.dot_general(masked, hours, (((0,), (0,)), ((), ())), preferred_element_type=F32)
    for scen in range(scens):
        rows[pl.ds(scen, total, stride=scens), :] = result[:, width * scen : width * (scen + 1)]
    for zone in range(zones):
        out[zone] = rows[count * zone : count * (zone + 1), :].astype(BF16)


def network_body(skip, place, links, scaled, *rest):
    parts, (out, weights, sems) = rest[:-3], rest[-3:]
    zones = out.shape[0]
    piece = parts[0].shape[1]
    half = len(parts) // 2
    copies = []
    for n, part in enumerate(parts):
        core = place[1] if n < half else 1 - place[1]
        y = lax.rem(place[0] + (n % half), half)
        first = pl.multiple_of((core * half + y) * piece, 16)
        copy = pltpu.make_async_copy(part, weights.at[:, pl.ds(first, piece), :], sems.at[n])
        copy.start()
        copies.append(copy)
    for copy in copies:
        copy.wait()
    for zone in range(zones):
        picked = jnp.concatenate(
            [scaled[links[zone, k], skip:, :] for k in range(links.shape[1])], axis=1
        )
        out[zone] = jnp.dot(picked, weights[zone], preferred_element_type=F32)


def combine_body(cot, step, grad0, network, temporal, adjoint, scaled, grad, rows):
    hours, scens, buses = cot.shape
    zones, count, width = scaled.shape
    for hour in range(hours):
        rows[scens * hour : scens * (hour + 1), :] = cot[hour]
    grad[...] = jnp.zeros_like(grad)
    for zone in range(zones):
        lanes = slice(width * zone, width * (zone + 1))
        value = rows[:, lanes] - network[zone] - temporal[zone].astype(F32)
        adjoint[zone] = value
        scaled[zone] = (value * step[:, lanes]).astype(BF16)
        summed = adjoint[zone, pl.ds(0, hours, stride=scens), :]
        for scen in range(1, scens):
            summed = summed + adjoint[zone, pl.ds(scen, hours, stride=scens), :]
        grad[zone, 0:hours, :] = summed * step[:, lanes] + grad0[:, lanes]


def finish_body(adjoint, network, temporal, out):
    hours, scens, buses = out.shape
    zones, count, width = temporal.shape
    for zone in range(zones):
        value = adjoint[zone] - network[zone] - temporal[zone].astype(F32)
        for hour in range(hours):
            out[hour, :, width * zone : width * (zone + 1)] = value[scens * hour : scens * (hour + 1)]


def siting_body(factor, place, parts, columns, out):
    hours, width = out.shape
    total = parts[0]
    for n in range(1, parts.shape[0]):
        total = total + parts[n]
    wanted = columns[...] - place[2] * width
    pick = (lax.broadcasted_iota(jnp.int32, (width, width), 0) == wanted).astype(F32)
    moved = jnp.dot(total * factor, pick, preferred_element_type=F32, precision=lax.Precision.HIGHEST)
    out[...] = moved[0:hours]


def ring(size, shift):
    return [(k, (k + shift) % size) for k in range(size)]


def per_device(cotangent, blocks, zone_links, step_size, coupling, ramp_band, candidates):
    scens, hours, buses = cotangent.shape
    zones, width = zone_links.shape[0], blocks.shape[3]
    count = hours * scens
    y, core = lax.axis_index("y"), lax.axis_index("core")
    size_y = lax.axis_size("y")
    piece = blocks.shape[1] * width // (2 * size_y)
    place = jnp.stack([core * size_y + y, y, core, lax.axis_index(SCEN)]).astype(jnp.int32)
    cot = jnp.transpose(cotangent, (1, 0, 2))
    step = step_size.reshape(1, buses)
    flat_blocks = blocks.reshape(blocks.shape[1] * width, width)
    sds = jax.ShapeDtypeStruct

    sent, grad0 = call(
        scale_body,
        (sds((zones, piece + count, width), BF16), sds((hours, buses), F32)),
        [pltpu.VMEM((count, buses), F32)],
        [SM, VM, VM, VM],
    )(place, cot, step, flat_blocks)
    got = lax.all_to_all(sent, TM, 0, 0, tiled=True)
    mine = got[:, 0:piece, :]
    near = [mine] + [lax.ppermute(mine, "y", ring(size_y, -d)) for d in range(1, size_y)]
    far = [lax.ppermute(part, "core", [(0, 1), (1, 0)]) for part in near]
    parts = near + far

    def temporal_of(skip, value):
        made = call(
            lambda *refs: temporal_body(skip, *refs),
            sds((zones, count, width), BF16),
            [pltpu.VMEM((zones * count, width), F32)],
            [SM, VM, VM],
        )(ramp_band, value, coupling[0])
        return lax.all_to_all(made, TM, 0, 0, tiled=True)

    def network_of(skip, value):
        return call(
            lambda *refs: network_body(skip, *refs),
            sds((zones, count, width), F32),
            [pltpu.VMEM((zones, blocks.shape[1] * width, width), BF16), pltpu.SemaphoreType.DMA((len(parts),))],
            [SM, SM, VM] + [ANY] * len(parts),
        )(place[1:3], zone_links, value, *parts)

    temporal = temporal_of(piece, got)
    network = network_of(piece, sent)
    adjoint, scaled, grad = call(
        combine_body,
        (sds((zones, count, width), F32), sds((zones, count, width), BF16), sds((zones, 24, width), F32)),
        [pltpu.VMEM((count, buses), F32)],
        [VM] * 5,
    )(cot, step, grad0, network, temporal)
    moved = lax.all_to_all(scaled, TM, 0, 0, tiled=True)
    temporal = temporal_of(0, moved)
    network = network_of(0, scaled)
    pieces = lax.all_to_all(grad, SCEN, 0, 0, tiled=True)
    factor = 1.0 / (scens * lax.axis_size(SCEN))
    siting = call(
        lambda *refs: siting_body(factor, *refs), sds((hours, width), F32), [], [SM, VM, VM]
    )(place[1:4], pieces, candidates.reshape(1, width))
    out = call(finish_body, sds((hours, scens, buses), F32), [], [VM] * 3)(adjoint, network, temporal)
    return jnp.transpose(out, (1, 0, 2)), siting


def solution(mesh):
    fine = Mesh(mesh.devices.reshape(2, 4, 2, 4, 4), SCEN + TM)
    placed = (
        P(SCEN, TM, None),
        P(TM, None, None, None),
        P(),
        P(),
        P(TM, None, None),
        P(TM),
        P(SCEN),
    )
    return jax.shard_map(
        per_device,
        mesh=fine,
        in_specs=placed,
        out_specs=(P(SCEN, TM, None), P(TM, SCEN)),
        check_vma=False,
    )
```

```python
import jax
import jax.numpy as jnp
from jax import lax
from jax.experimental import pallas as pl
from jax.experimental.pallas import tpu as pltpu
from jax.sharding import Mesh
from jax.sharding import PartitionSpec as P


SCEN = ("z_lo", "y", "core")
TM = ("z_hi", "x")
F32, BF16 = jnp.float32, jnp.bfloat16
VMEM_LIMIT = 48 * 1024 * 1024
SM = pl.BlockSpec(memory_space=pltpu.SMEM)
ANY = pl.BlockSpec(memory_space=pl.ANY)
VM = pl.BlockSpec()
SLOT = 96
NEXT = 88
NT = (((1,), (1,)), ((), ()))


def call(body, outs, specs, scratch=()):
    return pl.pallas_call(
        body,
        out_shape=outs,
        in_specs=specs,
        scratch_shapes=list(scratch),
        compiler_params=pltpu.CompilerParams(vmem_limit_bytes=VMEM_LIMIT),
    )


def strip_body(place, blocks, sent):
    count, width = sent.shape[1], blocks.shape[1]
    pick = (
        lax.broadcasted_iota(jnp.int32, (count, width), 1)
        == lax.broadcasted_iota(jnp.int32, (count, width), 0) + place[0] * count
    ).astype(F32).astype(BF16)
    own = lax.dot_general(pick, blocks[...], NT, preferred_element_type=F32).astype(BF16)
    for zone in range(sent.shape[0]):
        sent[zone] = own


def scenario_sum(rows, zone, hours, scens):
    total = rows[zone, pl.ds(0, hours, stride=scens), :]
    for scen in range(1, scens):
        total = total + rows[zone, pl.ds(scen, hours, stride=scens), :]
    return total


def scale_body(cot, step, scaled, rows):
    hours, scens, _ = cot.shape
    zones, _, width = scaled.shape
    for hour in range(hours):
        rows[scens * hour : scens * (hour + 1), :] = cot[hour] * step[...]
    for zone in range(zones):
        scaled[zone] = rows[:, width * zone : width * (zone + 1)].astype(BF16)


def strip_network_body(place, links, own, other, *rest):
    near = own.shape[1]
    size = (len(rest) - 3) // 2
    panels, outs, (gathered, weights, sems) = rest[:size], rest[size : 2 * size], rest[2 * size :]
    zones, count, width = gathered.shape[0], panels[0].shape[1], gathered.shape[2]
    copies = [
        pltpu.make_async_copy(panel, gathered.at[:, pl.ds(SLOT * n, count), :], sems.at[n])
        for n, panel in enumerate(panels)
    ]
    for copy in copies:
        copy.start()
    mine = pl.multiple_of(place[1] * near, 16)
    theirs = pl.multiple_of((1 - place[1]) * near, 16)
    weights[...] = jnp.zeros_like(weights)
    for zone in range(zones):
        base = 2 * near * zone
        for k in range(links.shape[1]):
            lanes = slice(width * k, width * (k + 1))
            weights[links[zone, k], pl.ds(base + mine, near), :] = own[zone, :, lanes]
            weights[links[zone, k], pl.ds(base + theirs, near), :] = other[zone, :, lanes]
    for copy in copies:
        copy.wait()
    panel = jnp.concatenate([gathered[zone] for zone in range(zones)], axis=1)
    step = 256
    for first in range(0, weights.shape[1], step):
        block = jnp.concatenate([weights[zone, first : first + step, :] for zone in range(zones)], axis=1)
        total = lax.dot_general(panel, block, NT, preferred_element_type=F32)
        for n in range(size):
            outs[n][:, first : first + step] = total[SLOT * n : SLOT * n + count].astype(BF16)


def masked_of(band, coupling):
    total = coupling.shape[0]
    spread = jnp.abs(
        lax.broadcasted_iota(jnp.int32, (total, total), 0)
        - lax.broadcasted_iota(jnp.int32, (total, total), 1)
    )
    return jnp.where(spread <= band[0], coupling[...].astype(F32), 0.0).astype(BF16)


def apply_temporal(band, coupling, rows, scens):
    total, width = coupling.shape[0], rows.shape[1]
    hours = jnp.concatenate(
        [rows[pl.ds(scen, total, stride=scens), :].astype(BF16) for scen in range(scens)], axis=1
    )
    result = lax.dot_general(
        masked_of(band, coupling), hours, (((0,), (0,)), ((), ())), preferred_element_type=F32
    )
    parts = [result[:, width * scen : width * (scen + 1)] for scen in range(scens)]
    for scen in range(scens):
        rows[pl.ds(scen, total, stride=scens), :] = parts[scen]
    return sum(parts[1:], parts[0])


def first_temporal_body(place, band, got, coupling, *rest):
    size = len(rest) - 5
    strips, (out, network, summed, rows, stack) = rest[:size], rest[size:]
    zones, count, width = got.shape
    scens = zones * count // coupling.shape[0]
    for zone in range(zones):
        rows[count * zone : count * (zone + 1), :] = got[zone].astype(F32)
    summed[...] = apply_temporal(band, coupling, rows, scens)
    for zone in range(zones):
        out[zone, 0:count, :] = rows[count * zone : count * (zone + 1), :].astype(BF16)
    for n in range(size):
        stack[lax.rem(place[0] + size - n, size)] = strips[n][...].astype(F32)
    wide = width // size
    lane = lax.broadcasted_iota(jnp.int32, (count, width), 1) // wide
    for zone in range(zones):
        first = width * (zone * wide // width)
        at = zone * wide % width // wide
        total = None
        for n in range(size):
            part = stack[n, :, first : first + width]
            if n != at:
                part = pltpu.roll(part, (n - at) % size * wide, 1)
            total = part if total is None else jnp.where(lane == n, part, total)
        value = total.astype(BF16)
        network[zone] = value
        out[zone, NEXT : NEXT + count, :] = value


def second_temporal_body(place, band, got, sent, back, coupling, step, out, rows):
    zones, count, _ = got.shape
    scens = zones * count // coupling.shape[0]
    own = step[pl.ds(place[3], 1), :]
    for zone in range(zones):
        both = sent[zone, 0:count, :].astype(F32) + back[zone, NEXT : NEXT + count, :].astype(F32)
        rows[count * zone : count * (zone + 1), :] = got[zone].astype(F32) - own * both
    apply_temporal(band, coupling, rows, scens)
    for zone in range(zones):
        out[zone] = rows[count * zone : count * (zone + 1), :].astype(BF16)


def sums_body(place, cot, network, summed, steps, *rest):
    outs, rows = rest[:-1], rest[-1]
    hours, scens, _ = cot.shape
    _, _, width = network.shape
    size = len(outs)
    part = outs[0].shape[1] // 2
    own = steps[pl.ds(place[3], 1), :]
    for d, out in enumerate(outs):
        y = lax.rem(place[2] + d, size)
        for n in range(4):
            zone = (n // 2) * (2 * size) + 2 * y + n % 2
            lanes = pl.ds(pl.multiple_of(zone * width, width), width)
            rows[n + 4 * d] = network[zone].astype(F32)
            total = 2.0 * jnp.sum(cot[:, :, lanes], axis=1) - scenario_sum(rows, n + 4 * d, hours, scens)
            out[n, 0:hours, :] = total * steps[pl.ds(zone, 1), :]
            out[n, hours:part, :] = jnp.zeros((part - hours, width), F32)
            out[n, part : part + hours, :] = -summed[zone] * own
            out[n, part + hours :, :] = jnp.zeros((part - hours, width), F32)


def network_body(place, links, cot, step, network, back, *rest):
    parts, (out, weights, rows, scaled, sems) = rest[:-5], rest[-5:]
    zones, near = out.shape[0], parts[0].shape[1]
    hours, scens, _ = cot.shape
    count, width = out.shape[1], out.shape[2]
    half = len(parts) // 2
    copies = []
    for n, part in enumerate(parts):
        core = place[1] if n < half else 1 - place[1]
        y = lax.rem(place[2] + (n % half), half)
        first = pl.multiple_of((y * 2 + core) * near, 16)
        copy = pltpu.make_async_copy(part, weights.at[:, pl.ds(first, near), :], sems.at[n])
        copy.start()
        copies.append(copy)
    for hour in range(hours):
        rows[scens * hour : scens * (hour + 1), :] = cot[hour]
    for zone in range(zones):
        lanes = slice(width * zone, width * (zone + 1))
        value = rows[:, lanes] - network[zone].astype(F32) - back[zone, 0:count, :].astype(F32)
        scaled[zone] = (value * step[:, lanes]).astype(BF16)
        out[zone] = value
    for copy in copies:
        copy.wait()
    for zone in range(zones):
        picked = jnp.concatenate([scaled[links[zone, k]] for k in range(links.shape[1])], axis=1)
        out[zone] = out[zone] - lax.dot_general(picked, weights[zone], NT, preferred_element_type=F32)


def finish_body(base, temporal, out):
    hours, scens, _ = out.shape
    zones, _, width = temporal.shape
    for zone in range(zones):
        value = base[zone] - temporal[zone].astype(F32)
        for hour in range(hours):
            out[hour, :, width * zone : width * (zone + 1)] = value[scens * hour : scens * (hour + 1)]


def siting_body(factor, place, kept, turned, columns, out):
    hours, width = out.shape
    wanted = columns[...] - place[4] * width
    pick = (lax.broadcasted_iota(jnp.int32, (width, width), 0) == wanted).astype(F32)
    total = (kept[...] + turned[...]) * factor
    moved = jnp.dot(total, pick, preferred_element_type=F32, precision=lax.Precision.HIGHEST)
    out[...] = moved[0:hours]


def ring(size, shift):
    return [(k, (k + shift) % size) for k in range(size)]


def exchange(array):
    return lax.all_to_all(array, TM, 0, 0, tiled=True)


def per_device(cotangent, blocks, zone_links, step_size, coupling, ramp_band, candidates):
    scens, hours, buses = cotangent.shape
    zones, width = zone_links.shape[0], blocks.shape[3]
    count, depth = hours * scens, blocks.shape[1] * width
    z_lo, y, core = (lax.axis_index(name) for name in SCEN)
    size_y = lax.axis_size("y")
    near = width // (2 * size_y)
    swap = [(0, 1), (1, 0)]
    place = jnp.stack([2 * y + core, core, y, lax.axis_index(TM), lax.axis_index(SCEN), z_lo]).astype(jnp.int32)
    cot = jnp.transpose(cotangent, (1, 0, 2))
    step = step_size.reshape(1, buses)
    sds = jax.ShapeDtypeStruct
    panel = sds((zones, count, width), BF16)
    wide_panel = sds((zones, count, width), F32)
    row_scratch = pltpu.VMEM((zones * count, width), F32)

    strips = call(strip_body, sds((zones, near, depth), BF16), [SM, VM])(
        place, blocks.reshape(depth, width)
    )
    own = exchange(strips)
    scaled0 = call(scale_body, panel, [VM, VM], [pltpu.VMEM((count, buses), F32)])(cot, step)
    panels = [scaled0] + [lax.ppermute(scaled0, "y", ring(size_y, -d)) for d in range(1, size_y)]
    other = lax.ppermute(own, "core", swap)
    got = exchange(scaled0)

    flat = sds((count, zones * width // size_y), BF16)
    made = call(
        strip_network_body,
        [flat] * size_y,
        [SM, SM, VM, VM] + [ANY] * size_y,
        [
            pltpu.VMEM((zones, SLOT * size_y, width), BF16),
            pltpu.VMEM((zones, zones * width // size_y, width), BF16),
            pltpu.SemaphoreType.DMA((size_y,)),
        ],
    )(place, zone_links, own, other, *panels)
    home = [made[0]] + [lax.ppermute(made[d], "y", ring(size_y, d)) for d in range(1, size_y)]

    sent, network0, summed = call(
        first_temporal_body,
        (sds((zones, NEXT + count, width), BF16), panel, sds((coupling.shape[1], width), F32)),
        [SM, SM, VM, VM] + [VM] * size_y,
        [row_scratch, pltpu.VMEM((size_y, count, zones * width // size_y), F32)],
    )(place[2:3], ramp_band, got, coupling[0], *home)
    back = exchange(sent)

    near_parts = [own] + [lax.ppermute(own, "y", ring(size_y, -d)) for d in range(1, size_y)]
    far_parts = [other] + [lax.ppermute(part, "core", swap) for part in near_parts[1:]]
    parts = near_parts + far_parts

    temporal1 = call(second_temporal_body, panel, [SM, SM] + [VM] * 5, [row_scratch])(
        place, ramp_band, got, sent, back, coupling[0], step_size.reshape(zones, width)
    )
    returned = exchange(temporal1)
    split = call(
        sums_body,
        [sds((4, 48, width), F32)] * size_y,
        [SM] + [VM] * 4,
        [pltpu.VMEM((zones, count, width), F32)],
    )(place, cot, network0, summed.reshape(zones, hours, width), step_size.reshape(zones, width))
    total = split[0]
    for d in range(1, size_y):
        total = total + lax.ppermute(split[d], "y", ring(size_y, d))
    total = total.reshape(2, 2, 48, width)
    total = total[:, core] + lax.ppermute(total[:, 1 - core], "core", swap)
    away = lax.ppermute(total[1 - z_lo], "z_lo", swap)
    total = total[z_lo] + away
    turned = lax.ppermute(
        total[24:], SCEN + TM, [(m * zones + z, z * zones + m) for m in range(zones) for z in range(zones)]
    )
    factor = 1.0 / (scens * lax.axis_size(SCEN))
    siting = call(
        lambda *refs: siting_body(factor, *refs), sds((hours, width), F32), [SM, VM, VM, VM]
    )(place, total[:24], turned, candidates.reshape(1, width))

    base = call(
        network_body,
        wide_panel,
        [SM, SM] + [VM] * 4 + [ANY] * len(parts),
        [
            pltpu.VMEM((zones, width, depth), BF16),
            pltpu.VMEM((count, buses), F32),
            pltpu.VMEM((zones, count, width), BF16),
            pltpu.SemaphoreType.DMA((len(parts),)),
        ],
    )(place, zone_links, cot, step, network0, back, *parts)
    out = call(finish_body, sds((hours, scens, buses), F32), [VM] * 2)(base, returned)
    return jnp.transpose(out, (1, 0, 2)), siting


def solution(mesh):
    fine = Mesh(mesh.devices.reshape(2, 4, 2, 4, 4), SCEN + TM)
    placed = (
        P(SCEN, TM, None),
        P(TM, None, None, None),
        P(),
        P(),
        P(TM, None, None),
        P(TM),
        P(SCEN),
    )
    return jax.shard_map(
        per_device,
        mesh=fine,
        in_specs=placed,
        out_specs=(P(SCEN, TM, None), P(TM, SCEN)),
        check_vma=False,
    )
```

```python
import jax
import jax.numpy as jnp
from jax import lax
from jax.experimental import pallas as pl
from jax.experimental.pallas import tpu as pltpu
from jax.sharding import Mesh
from jax.sharding import PartitionSpec as P


SCEN = ("z_lo", "y", "core")
TM = ("z_hi", "x")
F32, BF16 = jnp.float32, jnp.bfloat16
VMEM_LIMIT = 48 * 1024 * 1024
SM = pl.BlockSpec(memory_space=pltpu.SMEM)
ANY = pl.BlockSpec(memory_space=pl.ANY)
VM = pl.BlockSpec()
SLOT = 96
NEXT = 88
NT = (((1,), (1,)), ((), ()))


def call(body, outs, specs, scratch=()):
    return pl.pallas_call(
        body,
        out_shape=outs,
        in_specs=specs,
        scratch_shapes=list(scratch),
        compiler_params=pltpu.CompilerParams(vmem_limit_bytes=VMEM_LIMIT),
    )


def strip_body(place, blocks, sent):
    count, width = sent.shape[1], blocks.shape[1]
    pick = (
        lax.broadcasted_iota(jnp.int32, (count, width), 1)
        == lax.broadcasted_iota(jnp.int32, (count, width), 0) + place[0] * count
    ).astype(F32).astype(BF16)
    own = lax.dot_general(pick, blocks[...], NT, preferred_element_type=F32).astype(BF16)
    for zone in range(sent.shape[0]):
        sent[zone] = own


def scenario_sum(rows, zone, hours, scens):
    total = rows[zone, pl.ds(0, hours, stride=scens), :]
    for scen in range(1, scens):
        total = total + rows[zone, pl.ds(scen, hours, stride=scens), :]
    return total


def scale_body(cot, step, scaled, rows):
    hours, scens, _ = cot.shape
    zones, _, width = scaled.shape
    for hour in range(hours):
        rows[scens * hour : scens * (hour + 1), :] = cot[hour] * step[...]
    for zone in range(zones):
        scaled[zone] = rows[:, width * zone : width * (zone + 1)].astype(BF16)


def strip_network_body(place, links, own, other, *rest):
    near = own.shape[1]
    size = (len(rest) - 3) // 2
    panels, outs, (gathered, weights, sems) = rest[:size], rest[size : 2 * size], rest[2 * size :]
    zones, count, width = gathered.shape[0], panels[0].shape[1], gathered.shape[2]
    copies = [
        pltpu.make_async_copy(panel, gathered.at[:, pl.ds(SLOT * n, count), :], sems.at[n])
        for n, panel in enumerate(panels)
    ]
    for copy in copies:
        copy.start()
    mine = pl.multiple_of(place[1] * near, 16)
    theirs = pl.multiple_of((1 - place[1]) * near, 16)
    weights[...] = jnp.zeros_like(weights)
    for zone in range(zones):
        base = 2 * near * zone
        for k in range(links.shape[0]):
            lanes = slice(width * k, width * (k + 1))
            weights[links[k, zone], pl.ds(base + mine, near), :] = own[zone, :, lanes]
            weights[links[k, zone], pl.ds(base + theirs, near), :] = other[zone, :, lanes]
    for copy in copies:
        copy.wait()
    panel = jnp.concatenate([gathered[zone] for zone in range(zones)], axis=1)
    step = 256
    for first in range(0, weights.shape[1], step):
        block = jnp.concatenate([weights[zone, first : first + step, :] for zone in range(zones)], axis=1)
        total = lax.dot_general(panel, block, NT, preferred_element_type=F32)
        for n in range(size):
            outs[n][:, first : first + step] = total[SLOT * n : SLOT * n + count].astype(BF16)


def masked_of(band, coupling):
    total = coupling.shape[0]
    spread = jnp.abs(
        lax.broadcasted_iota(jnp.int32, (total, total), 0)
        - lax.broadcasted_iota(jnp.int32, (total, total), 1)
    )
    return jnp.where(spread <= band[0], coupling[...].astype(F32), 0.0).astype(BF16)


def apply_temporal(band, coupling, rows, scens):
    total, width = coupling.shape[0], rows.shape[1]
    hours = jnp.concatenate(
        [rows[pl.ds(scen, total, stride=scens), :].astype(BF16) for scen in range(scens)], axis=1
    )
    result = lax.dot_general(
        masked_of(band, coupling), hours, (((0,), (0,)), ((), ())), preferred_element_type=F32
    )
    parts = [result[:, width * scen : width * (scen + 1)] for scen in range(scens)]
    for scen in range(scens):
        rows[pl.ds(scen, total, stride=scens), :] = parts[scen]
    return sum(parts[1:], parts[0])


def first_temporal_body(place, band, got, coupling, *rest):
    size = len(rest) - 5
    strips, (out, network, summed, rows, stack) = rest[:size], rest[size:]
    zones, count, width = got.shape
    scens = zones * count // coupling.shape[0]
    for zone in range(zones):
        rows[count * zone : count * (zone + 1), :] = got[zone].astype(F32)
    summed[...] = apply_temporal(band, coupling, rows, scens)
    for zone in range(zones):
        out[zone, 0:count, :] = rows[count * zone : count * (zone + 1), :].astype(BF16)
    for n in range(size):
        stack[lax.rem(place[0] + size - n, size)] = strips[n][...].astype(F32)
    wide = width // size
    lane = lax.broadcasted_iota(jnp.int32, (count, width), 1) // wide
    for zone in range(zones):
        first = width * (zone * wide // width)
        at = zone * wide % width // wide
        total = None
        for n in range(size):
            part = stack[n, :, first : first + width]
            if n != at:
                part = pltpu.roll(part, (n - at) % size * wide, 1)
            total = part if total is None else jnp.where(lane == n, part, total)
        value = total.astype(BF16)
        network[zone] = value
        out[zone, NEXT : NEXT + count, :] = value


def second_temporal_body(place, band, got, sent, back, coupling, step, out, rows, come, sem):
    zones, count, _ = got.shape
    scens = zones * count // coupling.shape[0]
    copy = pltpu.make_async_copy(back.at[:, pl.ds(NEXT, count), :], come, sem)
    copy.start()
    own = step[pl.ds(place[3], 1), :]
    for zone in range(zones):
        value = got[zone].astype(F32) - own * sent[zone, 0:count, :].astype(F32)
        rows[count * zone : count * (zone + 1), :] = value
    copy.wait()
    for zone in range(zones):
        lines = slice(count * zone, count * (zone + 1))
        rows[lines, :] = rows[lines, :] - own * come[zone].astype(F32)
    apply_temporal(band, coupling, rows, scens)
    for zone in range(zones):
        out[zone] = rows[count * zone : count * (zone + 1), :].astype(BF16)


def sums_body(place, cot, network, summed, steps, *rest):
    outs, rows = rest[:-1], rest[-1]
    hours, scens, _ = cot.shape
    _, _, width = network.shape
    size = len(outs)
    part = outs[0].shape[1] // 2
    own = steps[pl.ds(place[3], 1), :]
    for d, out in enumerate(outs):
        y = lax.rem(place[2] + d, size)
        for n in range(4):
            zone = (n // 2) * (2 * size) + 2 * y + n % 2
            lanes = pl.ds(pl.multiple_of(zone * width, width), width)
            rows[n + 4 * d] = network[zone].astype(F32)
            total = 2.0 * jnp.sum(cot[:, :, lanes], axis=1) - scenario_sum(rows, n + 4 * d, hours, scens)
            out[n, 0:hours, :] = total * steps[pl.ds(zone, 1), :]
            out[n, hours:part, :] = jnp.zeros((part - hours, width), F32)
            out[n, part : part + hours, :] = -summed[zone] * own
            out[n, part + hours :, :] = jnp.zeros((part - hours, width), F32)


def network_body(place, links, cot, step, network, back, *rest):
    parts, (out, weights, rows, scaled, sems) = rest[:-5], rest[-5:]
    zones, near = out.shape[0], parts[0].shape[1]
    hours, scens, _ = cot.shape
    count, width = out.shape[1], out.shape[2]
    half = len(parts) // 2
    copies = []
    for n, part in enumerate(parts):
        core = place[1] if n < half else 1 - place[1]
        y = lax.rem(place[2] + (n % half), half)
        first = pl.multiple_of((y * 2 + core) * near, 16)
        copy = pltpu.make_async_copy(part, weights.at[:, pl.ds(first, near), :], sems.at[n])
        copy.start()
        copies.append(copy)
    for hour in range(hours):
        rows[scens * hour : scens * (hour + 1), :] = cot[hour]
    for zone in range(zones):
        lanes = slice(width * zone, width * (zone + 1))
        value = rows[:, lanes] - network[zone].astype(F32) - back[zone, 0:count, :].astype(F32)
        scaled[zone] = (value * step[:, lanes]).astype(BF16)
        out[zone] = value
    for copy in copies:
        copy.wait()
    for zone in range(zones):
        picked = jnp.concatenate([scaled[links[k, zone]] for k in range(links.shape[0])], axis=1)
        out[zone] = out[zone] - lax.dot_general(picked, weights[zone], NT, preferred_element_type=F32)


def finish_body(base, temporal, out):
    hours, scens, _ = out.shape
    zones, _, width = temporal.shape
    for zone in range(zones):
        value = base[zone] - temporal[zone].astype(F32)
        for hour in range(hours):
            out[hour, :, width * zone : width * (zone + 1)] = value[scens * hour : scens * (hour + 1)]


def siting_body(factor, place, kept, turned, columns, out):
    hours, width = out.shape
    wanted = columns[...] - place[4] * width
    pick = (lax.broadcasted_iota(jnp.int32, (width, width), 0) == wanted).astype(F32)
    total = (kept[...] + turned[...]) * factor
    moved = jnp.dot(total, pick, preferred_element_type=F32, precision=lax.Precision.HIGHEST)
    out[...] = moved[0:hours]


def ring(size, shift):
    return [(k, (k + shift) % size) for k in range(size)]


def exchange(array):
    return lax.all_to_all(array, TM, 0, 0, tiled=True)


def per_device(cotangent, blocks, zone_links, step_size, coupling, ramp_band, candidates):
    scens, hours, buses = cotangent.shape
    zones, width = zone_links.shape[0], blocks.shape[3]
    count, depth = hours * scens, blocks.shape[1] * width
    z_lo, y, core = (lax.axis_index(name) for name in SCEN)
    size_y = lax.axis_size("y")
    near = width // (2 * size_y)
    swap = [(0, 1), (1, 0)]
    place = jnp.stack([2 * y + core, core, y, lax.axis_index(TM), lax.axis_index(SCEN), z_lo]).astype(jnp.int32)
    cot = jnp.transpose(cotangent, (1, 0, 2))
    step = step_size.reshape(1, buses)
    sds = jax.ShapeDtypeStruct
    links = zone_links.T
    panel = sds((zones, count, width), BF16)
    wide_panel = sds((zones, count, width), F32)
    row_scratch = pltpu.VMEM((zones * count, width), F32)

    strips = call(strip_body, sds((zones, near, depth), BF16), [SM, VM])(
        place, blocks.reshape(depth, width)
    )
    own = exchange(strips)
    scaled0 = call(scale_body, panel, [VM, VM], [pltpu.VMEM((count, buses), F32)])(cot, step)
    panels = [scaled0] + [lax.ppermute(scaled0, "y", ring(size_y, -d)) for d in range(1, size_y)]
    other = lax.ppermute(own, "core", swap)
    got = exchange(scaled0)

    flat = sds((count, zones * width // size_y), BF16)
    made = call(
        strip_network_body,
        [flat] * size_y,
        [SM, SM, VM, VM] + [ANY] * size_y,
        [
            pltpu.VMEM((zones, SLOT * size_y, width), BF16),
            pltpu.VMEM((zones, zones * width // size_y, width), BF16),
            pltpu.SemaphoreType.DMA((size_y,)),
        ],
    )(place, links, own, other, *panels)
    home = [made[0]] + [lax.ppermute(made[d], "y", ring(size_y, d)) for d in range(1, size_y)]

    sent, network0, summed = call(
        first_temporal_body,
        (sds((zones, NEXT + count, width), BF16), panel, sds((coupling.shape[1], width), F32)),
        [SM, SM, VM, VM] + [VM] * size_y,
        [row_scratch, pltpu.VMEM((size_y, count, zones * width // size_y), F32)],
    )(place[2:3], ramp_band, got, coupling[0], *home)
    back = exchange(sent)

    near_parts = [own] + [lax.ppermute(own, "y", ring(size_y, -d)) for d in range(1, size_y)]
    far_parts = [other] + [lax.ppermute(part, "core", swap) for part in near_parts[1:]]
    parts = near_parts + far_parts

    temporal1 = call(
        second_temporal_body,
        panel,
        [SM, SM, VM, VM, ANY, VM, VM],
        [row_scratch, pltpu.VMEM((zones, count, width), BF16), pltpu.SemaphoreType.DMA],
    )(
        place, ramp_band, got, sent, back, coupling[0], step_size.reshape(zones, width)
    )
    returned = exchange(temporal1)
    split = call(
        sums_body,
        [sds((4, 48, width), F32)] * size_y,
        [SM] + [VM] * 4,
        [pltpu.VMEM((zones, count, width), F32)],
    )(place, cot, network0, summed.reshape(zones, hours, width), step_size.reshape(zones, width))
    total = split[0]
    for d in range(1, size_y):
        total = total + lax.ppermute(split[d], "y", ring(size_y, d))
    total = total.reshape(2, 2, 48, width)
    mine = total[z_lo]
    away = [
        lax.ppermute(total[1 - z_lo, core], "z_lo", swap),
        lax.ppermute(total[1 - z_lo, 1 - core], ("z_lo", "core"), [(n, 3 - n) for n in range(4)]),
        lax.ppermute(mine[1 - core], "core", swap),
    ]
    total = mine[core] + away[0] + away[1] + away[2]
    turned = lax.ppermute(
        total[24:], SCEN + TM, [(m * zones + z, z * zones + m) for m in range(zones) for z in range(zones)]
    )
    factor = 1.0 / (scens * lax.axis_size(SCEN))
    siting = call(
        lambda *refs: siting_body(factor, *refs), sds((hours, width), F32), [SM, VM, VM, VM]
    )(place, total[:24], turned, candidates.reshape(1, width))

    base = call(
        network_body,
        wide_panel,
        [SM, SM] + [VM] * 4 + [ANY] * len(parts),
        [
            pltpu.VMEM((zones, width, depth), BF16),
            pltpu.VMEM((count, buses), F32),
            pltpu.VMEM((zones, count, width), BF16),
            pltpu.SemaphoreType.DMA((len(parts),)),
        ],
    )(place, links, cot, step, network0, back, *parts)
    out = call(finish_body, sds((hours, scens, buses), F32), [VM] * 2)(base, returned)
    return jnp.transpose(out, (1, 0, 2)), siting


def solution(mesh):
    fine = Mesh(mesh.devices.reshape(2, 4, 2, 4, 4), SCEN + TM)
    placed = (
        P(SCEN, TM, None),
        P(TM, None, None, None),
        P(),
        P(),
        P(TM, None, None),
        P(TM),
        P(SCEN),
    )
    return jax.shard_map(
        per_device,
        mesh=fine,
        in_specs=placed,
        out_specs=(P(SCEN, TM, None), P(TM, SCEN)),
        check_vma=False,
    )
```
